32 devices in a mesh: seqmaj: 4 (over y, x), seqmin: 8 (over z, core).
Axes of the slice: x: 2, y: 2, z: 4, core: 2. Of those that a mesh axis runs over, the one named last changes fastest.
Arguments:
- q_first: bfloat16 [4096, 2048], P(('seqmaj', 'seqmin')), may hold values from -6 to 6
- k_first: bfloat16 [4096, 2048], P(('seqmaj', 'seqmin')), may hold values from -6 to 6
- v_first: bfloat16 [4096, 2048], P(('seqmaj', 'seqmin')), may hold values from -6 to 6
- mr_filter: bfloat16 [128, 2048], replicated, may hold values from -0.5 to 0.5
- mr_skip: float32 [2048], replicated, may hold values from -4 to 4
- value_weight: bfloat16 [2048, 2048], replicated, may hold values from -0.125 to 0.125
- q_second: bfloat16 [4096, 2048], P(('seqmaj', 'seqmin')), may hold values from -6 to 6
- k_second: bfloat16 [4096, 2048], P(('seqmaj', 'seqmin')), may hold values from -6 to 6
- li_residue: float32 [16, 2048], replicated, may hold values from -3 to 3
- li_rate: float32 [16, 2048], replicated, may hold values from 0.00012207031 to 0.033333335
- li_skip: float32 [2048], replicated, may hold values from -4 to 4
- out_second: bfloat16 [2048, 2048], replicated, may hold values from -0.0625 to 0.0625
Outputs:
- mixed: bfloat16 [4096, 2048], P(('seqmaj', 'seqmin'))
The draws below stay inside these ranges and needn't reach their ends.
All inputs are finite; a program needn't handle non-finite values.
Results may differ from the reference program's by a relative error of at most 0.015.
Values may be sent and summed in bfloat16 or wider, within the bound.
A program may use at most 128 MiB of HBM per device.

```python
import math
import jax
import jax.numpy as jnp
from jax import lax

C = 2048
MR_TAPS = 128
MODES = 16
TOKENS = 4096


def block_scale(stream_key, dims, pieces, low, top_value):
    factor_of, own = 1.0, jax.random.fold_in(stream_key, 6)
    for dim, blocks in pieces:
        steps = jnp.exp(jax.random.uniform(jax.random.fold_in(own, dim), (blocks,), jnp.float32, low / len(pieces), top_value / len(pieces)))
        factor_of = factor_of * jnp.repeat(steps, dims[dim] // blocks).reshape([-1 if axis == dim else 1 for axis in range(len(dims))])
    return factor_of


def scatter_about(stream_key, shape, scale, reach, split=(), dtype=jnp.bfloat16):
    drawn = scale * jax.random.normal(stream_key, shape, jnp.float32)
    if split:
        drawn = drawn * block_scale(stream_key, shape, split, -0.22, 0.18)
    return jnp.clip(drawn, -reach, reach).astype(dtype)


def setup_inputs(seed: int = 0) -> dict:
    key_of = jax.random.split(jax.random.key(seed), 13)
    return {
        "q_first": scatter_about(key_of[0], (TOKENS, C), 1.0, 6.0, ((0, 32),)),
        "k_first": scatter_about(key_of[1], (TOKENS, C), 1.0, 6.0, ((0, 32),)),
        "v_first": scatter_about(key_of[2], (TOKENS, C), 1.0, 6.0, ((0, 32),)),
        "mr_filter": scatter_about(key_of[3], (MR_TAPS, C), MR_TAPS ** -0.5, 0.5),
        "mr_skip": scatter_about(key_of[4], (C,), 1.0, 4.0, (), jnp.float32),
        "value_weight": scatter_about(key_of[5], (C, C), C ** -0.5, 0.125),
        "q_second": scatter_about(key_of[6], (TOKENS, C), 1.0, 6.0, ((0, 32),)),
        "k_second": scatter_about(key_of[7], (TOKENS, C), 1.0, 6.0, ((0, 32),)),
        "li_residue": scatter_about(key_of[8], (MODES, C), 0.5, 3.0, (), jnp.float32),
        "li_rate": jnp.clip(jnp.exp(jax.random.uniform(key_of[9], (MODES, C), jnp.float32, math.log(0.00012207031), math.log(0.033333335))), 0.00012207031, 0.033333335),
        "li_skip": scatter_about(key_of[10], (C,), 1.0, 4.0, (), jnp.float32),
        "out_second": scatter_about(key_of[11], (C, C), (4 * C) ** -0.5, 0.0625),
    }


def long_block(signal_block, residue_block, rate_block):
    times = jnp.arange(TOKENS).astype(jnp.float32)
    weight = residue_block * jnp.sqrt(rate_block)
    long_filter = lax.optimization_barrier(jnp.sum(weight[None, :, :] * jnp.exp(-rate_block[None, :, :] * times[:, None, None]), axis=1))
    padded_size = 2 * TOKENS
    product = jnp.fft.rfft(signal_block, n=padded_size, axis=0) * jnp.fft.rfft(long_filter, n=padded_size, axis=0)
    return jnp.fft.irfft(product, n=padded_size, axis=0)[:TOKENS]

def short_convolution(padded, taps):

    def add_tap(step, total):
        start = (MR_TAPS - 1 - step).astype(jnp.int32)
        piece = lax.dynamic_slice_in_dim(padded, start, TOKENS, 0)
        row = lax.dynamic_slice_in_dim(taps, step.astype(jnp.int32), 1, 0)
        return total + row * piece
    initial = jnp.zeros((TOKENS, C), jnp.float32)
    return lax.fori_loop(jnp.int32(0), jnp.int32(MR_TAPS), add_tap, initial)

def reference(q_first, k_first, v_first, mr_filter, mr_skip, value_weight, q_second, k_second, li_residue, li_rate, li_skip, out_second):
    gated_first = (k_first.astype(jnp.float32) * v_first.astype(jnp.float32)).astype(jnp.bfloat16)
    padded = jnp.concatenate([jnp.zeros((MR_TAPS - 1, C), jnp.float32), gated_first.astype(jnp.float32)], axis=0)
    short_conv = short_convolution(padded, mr_filter.astype(jnp.float32))
    first_act = (q_first.astype(jnp.float32) * (short_conv + mr_skip[None, :] * gated_first.astype(jnp.float32))).astype(jnp.bfloat16)
    v_second = jnp.dot(first_act, value_weight, preferred_element_type=jnp.float32).astype(jnp.bfloat16)
    gated_second = (k_second.astype(jnp.float32) * v_second.astype(jnp.float32)).astype(jnp.bfloat16)
    block_count = C // 16
    signal_blocks = jnp.moveaxis(gated_second.astype(jnp.float32).reshape(TOKENS, block_count, 16), 1, 0)
    residue_blocks = jnp.moveaxis(li_residue.reshape(MODES, block_count, 16), 1, 0)
    rate_blocks = jnp.moveaxis(li_rate.reshape(MODES, block_count, 16), 1, 0)
    conv_blocks = lax.map(lambda items: long_block(items[0], items[1], items[2]), (signal_blocks, residue_blocks, rate_blocks))
    long_conv = jnp.moveaxis(conv_blocks, 0, 1).reshape(TOKENS, C)
    second_act = (q_second.astype(jnp.float32) * (long_conv + li_skip[None, :] * gated_second.astype(jnp.float32))).astype(jnp.bfloat16)
    return jnp.dot(second_act, out_second, preferred_element_type=jnp.float32).astype(jnp.bfloat16)
```

```python
import jax
import jax.numpy as jnp
import numpy as np
from jax import lax
from jax.sharding import PartitionSpec as P

axes = ("seqmaj", "seqmin")


def dft_tables(rows):
    size = 2 * rows
    theta = 2.0 * np.pi * (np.arange(rows) + 0.5) / size
    angle = theta[:, None] * np.arange(size)[None, :]
    forward = np.concatenate([np.cos(angle), np.sin(angle)], axis=0)
    inverse = forward.T / rows
    return forward.astype(np.float32), inverse.astype(np.float32)


def mm(a, b):
    return jnp.dot(a.astype(jnp.bfloat16), b.astype(jnp.bfloat16), preferred_element_type=jnp.float32)


def spectral_product(x, h):
    n = x.shape[0] // 2
    xc, xs, hc, hs = x[:n], x[n:], h[:n], h[n:]
    return jnp.concatenate([xc * hc - xs * hs, xc * hs + xs * hc], axis=0)


def local(q1, k1, v1, taps, skip1, w1, q2, k2, residue, rate, skip2, w2):
    f32, bf16 = jnp.float32, jnp.bfloat16
    rows, channels = q1.shape
    modes = rate.shape[0]
    minor = lax.axis_size("seqmin")
    n = lax.axis_size("seqmaj") * minor
    fwd, inv = dft_tables(rows)
    g1 = (k1.astype(f32) * v1.astype(f32)).astype(bf16)
    border = lax.ppermute(g1, axes, [(i, i + 1) for i in range(n - 1)])
    window = jnp.concatenate([border, g1], axis=0)
    spec = spectral_product(mm(fwd, window), mm(fwd[:, :rows], taps))
    short = mm(inv[rows:], spec)
    act1 = (q1.astype(f32) * (short + skip1[None, :] * g1.astype(f32))).astype(bf16)
    v2 = jnp.dot(act1, w1, preferred_element_type=f32).astype(bf16)
    g2 = (k2.astype(f32) * v2.astype(f32)).astype(bf16)
    g2f = g2.astype(f32)
    t = jnp.arange(rows, dtype=f32)
    weight = residue * jnp.sqrt(rate)
    powers = jnp.exp(-rate[None] * t[:, None, None])
    head = jnp.sum(weight[None] * powers, axis=1)
    spec2 = spectral_product(mm(fwd[:, :rows], g2), mm(fwd[:, :rows], head))
    near = mm(inv[:rows], spec2)
    ends = jnp.sum(jnp.exp(-rate[None] * (rows - 1.0 - t)[:, None, None]) * g2f[:, None, :], axis=0)
    flat = modes * channels // n
    got = lax.all_to_all(ends.reshape(n, flat).astype(bf16), axes, 0, 0, tiled=True).astype(f32)
    device = lax.axis_index("seqmaj") * minor + lax.axis_index("seqmin")
    own_rate = lax.dynamic_index_in_dim(rate.reshape(n, flat), device, 0, keepdims=False)
    d = jnp.arange(n, dtype=f32)
    lag = d[:, None] - 1.0 - d[None, :]
    decay = jnp.where(lag[:, :, None] >= 0, jnp.exp(-own_rate * (rows * jnp.maximum(lag, 0.0))[:, :, None]), 0.0)
    carry = jnp.sum(decay * got[None], axis=1)
    state = lax.all_to_all(carry.astype(bf16), axes, 0, 0, tiled=True).astype(f32).reshape(modes, channels)
    far = jnp.sum((weight * state)[None] * jnp.exp(-rate[None] * (t + 1.0)[:, None, None]), axis=1)
    act2 = (q2.astype(f32) * (near + far + skip2[None, :] * g2f)).astype(bf16)
    return jnp.dot(act2, w2, preferred_element_type=f32).astype(bf16)


def solution(mesh):
    s, r = P(axes, None), P()
    specs = (s, s, s, r, r, r, s, s, r, r, r, r)
    return jax.shard_map(local, mesh=mesh, in_specs=specs, out_specs=s, check_vma=False)
```

```python
import functools

import jax
import jax.numpy as jnp
import numpy as np
from jax import lax
from jax.experimental import pallas as pl
from jax.experimental.pallas import tpu as pltpu
from jax.sharding import PartitionSpec as P

axes = ("seqmaj", "seqmin")
MESH = pl.DeviceIdType.MESH
f32, bf16 = jnp.float32, jnp.bfloat16
WIDE = 256
LANES = 128
SUB = 8


def dft_tables(rows):
    size = 2 * rows
    theta = 2.0 * np.pi * (np.arange(rows) + 0.5) / size
    angle = theta[:, None] * np.arange(size)[None, :]
    forward = np.concatenate([np.cos(angle), np.sin(angle)], axis=0)
    inverse = forward.T / rows
    return jnp.asarray(forward, bf16), jnp.asarray(inverse, bf16)


def mm(a, b):
    return jnp.dot(a, b, preferred_element_type=f32)


def spectral_product(x, h):
    half = x.shape[0] // 2
    xc, xs, hc, hs = x[:half], x[half:], h[:half], h[half:]
    return jnp.concatenate([xc * hc - xs * hs, xc * hs + xs * hc], axis=0).astype(bf16)


def kernel(
    n, minor, q1h, k1h, v1h, tapsh, skip1h, w1h, q2h, k2h, resh, rateh, skip2h, w2h, fwdh, invh, out,
    q1, k1, v1, taps, skip1, w1, q2, k2, res, rate, skip2, w2, fwd, inv,
    win, h1, h2, a8, p7, p1, head, acc, y, g2, ends, got, sout, sin, tiled_rate,
    in_sem, w1_sem, w2_sem, bsend, brecv, esend, erecv, ssend, srecv,
):
    rows, channels = q1.shape
    modes = rate.shape[0]
    chunks = channels // WIDE
    blocks = channels // LANES
    per_tile = n * SUB * LANES // (modes * channels)
    part = SUB // per_tile
    me = lax.axis_index("seqmaj") * minor + lax.axis_index("seqmin")

    def place(d):
        return (lax.div(d, minor), lax.rem(d, minor))

    def load(i, src, dst):
        return pltpu.make_async_copy(src, dst, in_sem.at[i])

    loads = {}
    for i, (name, src, dst) in enumerate([
        ("k1", k1h, k1), ("v1", v1h, v1), ("fwd", fwdh, fwd), ("taps", tapsh, taps), ("rate", rateh, rate),
        ("res", resh, res), ("inv", invh, inv), ("q1", q1h, q1), ("skip1", skip1h, skip1), ("k2", k2h, k2),
        ("skip2", skip2h, skip2), ("q2", q2h, q2),
    ]):
        loads[name] = load(i, src, dst)
        loads[name].start()

    def weight_load(src, dst, sem, c):
        span = pl.ds(pl.multiple_of(c * WIDE, WIDE), WIDE)
        return pltpu.make_async_copy(src.at[span, :], dst.at[span, :], sem.at[c])

    @pl.loop(0, chunks)
    def _(c):
        weight_load(w1h, w1, w1_sem, c).start()

    barrier = pltpu.get_barrier_semaphore()

    @pl.loop(1, n)
    def _(p):
        pl.semaphore_signal(barrier, inc=1, device_id=place(lax.rem(me + p, n)), device_id_type=MESH)

    @pl.loop(0, chunks)
    def _(c):
        weight_load(w2h, w2, w2_sem, c).start()

    def wide(c):
        return pl.ds(pl.multiple_of(c * WIDE, WIDE), WIDE)

    loads["k1"].wait()
    loads["v1"].wait()

    @pl.loop(0, chunks)
    def _(c):
        cols = wide(c)
        win[c, rows:, :] = (k1[:, cols].astype(f32) * v1[:, cols].astype(f32)).astype(bf16)

    pl.semaphore_wait(barrier, n - 1)

    def border(c):
        return pltpu.make_async_remote_copy(
            src_ref=win.at[c, pl.ds(rows, rows), :], dst_ref=win.at[c, pl.ds(0, rows), :],
            send_sem=bsend.at[c], recv_sem=brecv.at[c],
            device_id=place(lax.rem(me + 1, n)), device_id_type=MESH,
        )

    @pl.when(me < n - 1)
    def _():
        @pl.loop(0, chunks)
        def _(c):
            border(c).start()

    @pl.when(me == 0)
    def _():
        @pl.loop(0, chunks)
        def _(c):
            win[c, :rows, :] = jnp.zeros((rows, WIDE), bf16)

    loads["fwd"].wait()
    loads["taps"].wait()
    loads["rate"].wait()
    loads["res"].wait()
    step = lax.broadcasted_iota(jnp.int32, (modes, SUB, LANES), 1).astype(f32)

    def spread(ref, b):
        cols = pl.ds(pl.multiple_of(b * LANES, LANES), LANES)
        return jnp.stack([jnp.broadcast_to(ref[r : r + 1, cols], (SUB, LANES)) for r in range(modes)])

    @pl.loop(0, chunks)
    def _(c):
        h1[c] = mm(fwd[:, :rows], taps[:, wide(c)])
        for j in range(WIDE // LANES):
            b = c * (WIDE // LANES) + j
            lam = spread(rate, b)
            weight = spread(res, b) * jnp.sqrt(lam)
            decay = jnp.exp(-SUB * lam)
            a8[b] = decay
            lanes = rate[:, pl.ds(pl.multiple_of(b * LANES, LANES), LANES)]
            for hi in range(modes // SUB):
                for s in range(per_tile):
                    start = hi * SUB + s * part
                    tiled_rate[(hi * blocks + b) * per_tile + s] = lanes[start : start + part]
            p7[b] = jnp.exp(-lam * (SUB - 1.0 - step))
            p1[b] = weight * jnp.exp(-lam * (step + 1.0))
            u = weight * jnp.exp(-lam * step)
            for m in range(rows // SUB):
                head[m * SUB : (m + 1) * SUB, j * LANES : (j + 1) * LANES] = jnp.sum(u, axis=0)
                u = u * decay
        h2[c] = mm(fwd[:, :rows], head[...].astype(bf16))

    loads["inv"].wait()
    loads["q1"].wait()
    loads["skip1"].wait()
    acc[...] = jnp.zeros_like(acc)

    @pl.loop(0, chunks)
    def _(c):
        cols = wide(c)

        @pl.when(me > 0)
        def _():
            border(c).wait_recv()

        spec = spectral_product(mm(fwd[...], win[c]), h1[c])
        short = mm(inv[rows:, :], spec)
        own = win[c, rows:, :].astype(f32)
        act = (q1[:, cols].astype(f32) * (short + skip1[:, cols] * own)).astype(bf16)
        weight_load(w1h, w1, w1_sem, c).wait()
        acc[...] += mm(act, w1[cols, :])

    loads["k2"].wait()
    loads["skip2"].wait()

    def ends_copy(o):
        return pltpu.make_async_remote_copy(
            src_ref=ends.at[o], dst_ref=got.at[me], send_sem=esend.at[o], recv_sem=erecv.at[me],
            device_id=place(o), device_id_type=MESH,
        )

    @pl.loop(0, chunks)
    def _(i):
        c = lax.rem(i + me, chunks)
        cols = wide(c)
        gated = (k2[:, cols].astype(f32) * acc[:, cols].astype(bf16).astype(f32)).astype(bf16)
        g2[c] = gated
        for j in range(WIDE // LANES):
            b = c * (WIDE // LANES) + j
            g = gated[:, j * LANES : (j + 1) * LANES].astype(f32)
            decay = a8[b]
            h = jnp.broadcast_to(g[:SUB][None], (modes, SUB, LANES))
            for m in range(1, rows // SUB):
                h = h * decay + g[m * SUB : (m + 1) * SUB][None]
            e = jnp.sum(h * p7[b], axis=1)
            for hi in range(modes // SUB):
                for s in range(per_tile):
                    o = (hi * blocks + b) * per_tile + s
                    piece = e[hi * SUB + s * part : hi * SUB + (s + 1) * part]
                    ends[o] = piece

                    @pl.when(o != me)
                    def _():
                        ends_copy(o).start()

                    @pl.when(o == me)
                    def _():
                        got[me] = piece

    @pl.loop(0, chunks)
    def _(c):
        gated = g2[c]
        spec = spectral_product(mm(fwd[:, :rows], gated), h2[c])
        y[c] = mm(inv[:rows, :], spec) + skip2[:, wide(c)] * gated.astype(f32)

    @pl.loop(0, n)
    def _(d):
        @pl.when(d != me)
        def _():
            pltpu.make_async_remote_copy(
                src_ref=ends.at[d], dst_ref=got.at[d], send_sem=esend.at[d], recv_sem=erecv.at[d],
                device_id=place(d), device_id_type=MESH,
            ).wait_recv()

    own_decay = jnp.exp(-float(rows) * tiled_rate[me])

    def scan(d, state):
        sout[d] = state
        return state * own_decay + got[d]

    lax.fori_loop(0, n, scan, jnp.zeros((part, LANES), f32))

    def state_copy(d):
        return pltpu.make_async_remote_copy(
            src_ref=sout.at[d], dst_ref=sin.at[me], send_sem=ssend.at[d], recv_sem=srecv.at[me],
            device_id=place(d), device_id_type=MESH,
        )

    @pl.loop(1, n)
    def _(p):
        state_copy(lax.rem(me + p, n)).start()

    sin[me] = sout[me]
    loads["q2"].wait()

    @pl.loop(0, n)
    def _(d):
        @pl.when(d != me)
        def _():
            pltpu.make_async_remote_copy(
                src_ref=sout.at[d], dst_ref=sin.at[d], send_sem=ssend.at[d], recv_sem=srecv.at[d],
                device_id=place(d), device_id_type=MESH,
            ).wait_recv()

    acc[...] = jnp.zeros_like(acc)

    @pl.loop(0, chunks)
    def _(c):
        cols = wide(c)
        for j in range(WIDE // LANES):
            b = c * (WIDE // LANES) + j
            lane = slice(j * LANES, (j + 1) * LANES)
            state = []
            for r in range(modes):
                hi, low = divmod(r, SUB)
                s, row = divmod(low, part)
                o = (hi * blocks + b) * per_tile + s
                state.append(jnp.broadcast_to(sin[o, row : row + 1, :], (SUB, LANES)))
            u = p1[b] * jnp.stack(state)
            decay = a8[b]
            for m in range(rows // SUB):
                span = slice(m * SUB, (m + 1) * SUB)
                head[span, lane] = jnp.sum(u, axis=0)
                u = u * decay
        act = (q2[:, cols].astype(f32) * (y[c] + head[...])).astype(bf16)
        weight_load(w2h, w2, w2_sem, c).wait()
        acc[...] += mm(act, w2[cols, :])

    out[...] = acc[...].astype(bf16)

    @pl.when(me < n - 1)
    def _():
        @pl.loop(0, chunks)
        def _(c):
            border(c).wait_send()

    @pl.loop(0, n)
    def _(d):
        @pl.when(d != me)
        def _():
            ends_copy(d).wait_send()
            state_copy(d).wait_send()


def local(q1, k1, v1, taps, skip1, w1, q2, k2, residue, rate, skip2, w2):
    rows, channels = q1.shape
    modes = rate.shape[0]
    minor = lax.axis_size("seqmin")
    n = lax.axis_size("seqmaj") * minor
    fwd, inv = dft_tables(rows)
    operands = (q1, k1, v1, taps, skip1[None], w1, q2, k2, residue, rate, skip2[None], w2, fwd, inv)
    chunks, blocks = channels // WIDE, channels // LANES
    states = (n, modes * channels // (n * LANES), LANES)
    scratch = [pltpu.VMEM(a.shape, a.dtype) for a in operands] + [
        pltpu.VMEM((chunks, 2 * rows, WIDE), bf16),
        pltpu.VMEM((chunks, 2 * rows, WIDE), f32),
        pltpu.VMEM((chunks, 2 * rows, WIDE), f32),
        pltpu.VMEM((blocks, modes, SUB, LANES), f32),
        pltpu.VMEM((blocks, modes, SUB, LANES), f32),
        pltpu.VMEM((blocks, modes, SUB, LANES), f32),
        pltpu.VMEM((rows, WIDE), f32),
        pltpu.VMEM((rows, channels), f32),
        pltpu.VMEM((chunks, rows, WIDE), f32),
        pltpu.VMEM((chunks, rows, WIDE), bf16),
        pltpu.VMEM(states, f32),
        pltpu.VMEM(states, f32),
        pltpu.VMEM(states, f32),
        pltpu.VMEM(states, f32),
        pltpu.VMEM(states, f32),
        pltpu.SemaphoreType.DMA((12,)),
        pltpu.SemaphoreType.DMA((chunks,)),
        pltpu.SemaphoreType.DMA((chunks,)),
        pltpu.SemaphoreType.DMA((chunks,)),
        pltpu.SemaphoreType.DMA((chunks,)),
        pltpu.SemaphoreType.DMA((n,)),
        pltpu.SemaphoreType.DMA((n,)),
        pltpu.SemaphoreType.DMA((n,)),
        pltpu.SemaphoreType.DMA((n,)),
    ]
    return pl.pallas_call(
        functools.partial(kernel, n, minor),
        out_shape=jax.ShapeDtypeStruct((rows, channels), bf16),
        in_specs=[pl.BlockSpec(memory_space=pl.ANY)] * len(operands),
        out_specs=pl.BlockSpec(memory_space=pltpu.VMEM),
        scratch_shapes=scratch,
        compiler_params=pltpu.CompilerParams(
            collective_id=0, has_side_effects=True, vmem_limit_bytes=48 * 1024 * 1024
        ),
    )(*operands)


def solution(mesh):
    s, r = P(axes, None), P()
    specs = (s, s, s, r, r, r, s, s, r, r, r, r)
    return jax.shard_map(local, mesh=mesh, in_specs=specs, out_specs=s, check_vma=False)
```

```python
import functools

import jax
import jax.numpy as jnp
import numpy as np
from jax import lax
from jax.experimental import pallas as pl
from jax.experimental.pallas import tpu as pltpu
from jax.sharding import PartitionSpec as P

axes = ("seqmaj", "seqmin")
MESH = pl.DeviceIdType.MESH
f32, bf16 = jnp.float32, jnp.bfloat16
WIDE = 256
LANES = 128
SUB = 8


def dft_tables(rows):
    size = 2 * rows
    theta = 2.0 * np.pi * (np.arange(rows) + 0.5) / size
    angle = theta[:, None] * np.arange(size)[None, :]
    forward = np.concatenate([np.cos(angle), np.sin(angle)], axis=0)
    inverse = forward.T / rows
    return jnp.asarray(forward, bf16), jnp.asarray(inverse, bf16)


def mm(a, b):
    return jnp.dot(a, b, preferred_element_type=f32)


def spectral_product(x, h):
    half = x.shape[0] // 2
    xc, xs, hc, hs = x[:half], x[half:], h[:half], h[half:]
    return jnp.concatenate([xc * hc - xs * hs, xc * hs + xs * hc], axis=0).astype(bf16)


def kernel(
    n, minor, q1h, k1h, v1h, tapsh, skip1h, w1h, q2h, k2h, resh, rateh, skip2h, w2h, fwdh, invh, out,
    q1, k1, v1, taps, skip1, w1, q2, k2, res, rate, skip2, w2, fwd, inv,
    win, h1, h2, a8, p7, p1, head, acc, y, g2, ends, got, sout, sin, tiled_rate,
    in_sem, w1_sem, w2_sem, bsend, brecv, esend, erecv, ssend, srecv,
):
    rows, channels = q1.shape
    modes = rate.shape[0]
    chunks = channels // WIDE
    blocks = channels // LANES
    per_tile = n * SUB * LANES // (modes * channels)
    part = SUB // per_tile
    me = lax.axis_index("seqmaj") * minor + lax.axis_index("seqmin")

    def place(d):
        return (lax.div(d, minor), lax.rem(d, minor))

    def load(i, src, dst):
        return pltpu.make_async_copy(src, dst, in_sem.at[i])

    loads = {}
    for i, (name, src, dst) in enumerate([
        ("k1", k1h, k1), ("v1", v1h, v1), ("fwd", fwdh, fwd), ("taps", tapsh, taps), ("rate", rateh, rate),
        ("res", resh, res), ("inv", invh, inv), ("q1", q1h, q1), ("skip1", skip1h, skip1), ("k2", k2h, k2),
        ("skip2", skip2h, skip2), ("q2", q2h, q2),
    ]):
        loads[name] = load(i, src, dst)
        loads[name].start()

    def weight_load(src, dst, sem, c):
        span = pl.ds(pl.multiple_of(c * WIDE, WIDE), WIDE)
        return pltpu.make_async_copy(src.at[span, :], dst.at[span, :], sem.at[c])

    @pl.loop(0, chunks)
    def _(c):
        weight_load(w1h, w1, w1_sem, c).start()

    barrier = pltpu.get_barrier_semaphore()

    @pl.loop(1, n)
    def _(p):
        pl.semaphore_signal(barrier, inc=1, device_id=place(lax.rem(me + p, n)), device_id_type=MESH)

    @pl.loop(0, chunks)
    def _(c):
        weight_load(w2h, w2, w2_sem, c).start()

    def wide(c):
        return pl.ds(pl.multiple_of(c * WIDE, WIDE), WIDE)

    loads["k1"].wait()
    loads["v1"].wait()

    @pl.loop(0, chunks)
    def _(c):
        cols = wide(c)
        win[c, rows:, :] = (k1[:, cols].astype(f32) * v1[:, cols].astype(f32)).astype(bf16)

    pl.semaphore_wait(barrier, n - 1)

    def border(c):
        return pltpu.make_async_remote_copy(
            src_ref=win.at[c, pl.ds(rows, rows), :], dst_ref=win.at[c, pl.ds(0, rows), :],
            send_sem=bsend.at[c], recv_sem=brecv.at[c],
            device_id=place(lax.rem(me + 1, n)), device_id_type=MESH,
        )

    @pl.when(me < n - 1)
    def _():
        @pl.loop(0, chunks)
        def _(c):
            border(c).start()

    @pl.when(me == 0)
    def _():
        @pl.loop(0, chunks)
        def _(c):
            win[c, :rows, :] = jnp.zeros((rows, WIDE), bf16)

    loads["fwd"].wait()
    loads["taps"].wait()
    loads["rate"].wait()
    loads["res"].wait()
    step = lax.broadcasted_iota(jnp.int32, (modes, SUB, LANES), 1).astype(f32)

    def spread(ref, b):
        cols = pl.ds(pl.multiple_of(b * LANES, LANES), LANES)
        return jnp.stack([jnp.broadcast_to(ref[r : r + 1, cols], (SUB, LANES)) for r in range(modes)])

    @pl.loop(0, chunks)
    def _(c):
        h1[c] = mm(fwd[:, :rows], taps[:, wide(c)])
        for j in range(WIDE // LANES):
            b = c * (WIDE // LANES) + j
            lam = spread(rate, b)
            weight = spread(res, b) * jnp.sqrt(lam)
            decay = jnp.exp(-SUB * lam)
            a8[b] = decay
            lanes = rate[:, pl.ds(pl.multiple_of(b * LANES, LANES), LANES)]
            for hi in range(modes // SUB):
                for s in range(per_tile):
                    start = hi * SUB + s * part
                    tiled_rate[(hi * blocks + b) * per_tile + s] = lanes[start : start + part]
            p7[b] = jnp.exp(-lam * (SUB - 1.0 - step))
            p1[b] = weight * jnp.exp(-lam * (step + 1.0))
            u = weight * jnp.exp(-lam * step)
            for m in range(rows // SUB):
                head[m * SUB : (m + 1) * SUB, j * LANES : (j + 1) * LANES] = jnp.sum(u, axis=0)
                u = u * decay
        h2[c] = mm(fwd[:, :rows], head[...].astype(bf16))

    loads["inv"].wait()
    loads["q1"].wait()
    loads["skip1"].wait()
    acc[...] = jnp.zeros_like(acc)

    @pl.loop(0, chunks)
    def _(c):
        cols = wide(c)

        @pl.when(me > 0)
        def _():
            border(c).wait_recv()

        spec = spectral_product(mm(fwd[...], win[c]), h1[c])
        short = mm(inv[rows:, :], spec)
        own = win[c, rows:, :].astype(f32)
        act = (q1[:, cols].astype(f32) * (short + skip1[:, cols] * own)).astype(bf16)
        weight_load(w1h, w1, w1_sem, c).wait()
        acc[...] += mm(act, w1[cols, :])

    loads["k2"].wait()
    loads["skip2"].wait()

    def ends_copy(o):
        return pltpu.make_async_remote_copy(
            src_ref=ends.at[o], dst_ref=got.at[me], send_sem=esend.at[o], recv_sem=erecv.at[me],
            device_id=place(o), device_id_type=MESH,
        )

    @pl.loop(0, chunks)
    def _(i):
        c = lax.rem(i + me, chunks)
        cols = wide(c)
        gated = (k2[:, cols].astype(f32) * acc[:, cols].astype(bf16).astype(f32)).astype(bf16)
        g2[c] = gated
        for j in range(WIDE // LANES):
            b = c * (WIDE // LANES) + j
            g = gated[:, j * LANES : (j + 1) * LANES].astype(f32)
            decay = a8[b]
            h = jnp.broadcast_to(g[:SUB][None], (modes, SUB, LANES))
            for m in range(1, rows // SUB):
                h = h * decay + g[m * SUB : (m + 1) * SUB][None]
            e = jnp.sum(h * p7[b], axis=1)
            for hi in range(modes // SUB):
                for s in range(per_tile):
                    o = (hi * blocks + b) * per_tile + s
                    piece = e[hi * SUB + s * part : hi * SUB + (s + 1) * part]
                    ends[o] = piece

                    @pl.when(o != me)
                    def _():
                        ends_copy(o).start()

                    @pl.when(o == me)
                    def _():
                        got[me] = piece

    @pl.loop(0, chunks)
    def _(c):
        gated = g2[c]
        spec = spectral_product(mm(fwd[:, :rows], gated), h2[c])
        y[c] = mm(inv[:rows, :], spec) + skip2[:, wide(c)] * gated.astype(f32)

    @pl.loop(0, n)
    def _(d):
        @pl.when(d != me)
        def _():
            pltpu.make_async_remote_copy(
                src_ref=ends.at[d], dst_ref=got.at[d], send_sem=esend.at[d], recv_sem=erecv.at[d],
                device_id=place(d), device_id_type=MESH,
            ).wait_recv()

    own_decay = jnp.exp(-float(rows) * tiled_rate[me])

    def scan(d, state):
        sout[d] = state
        return state * own_decay + got[d]

    lax.fori_loop(0, n, scan, jnp.zeros((part, LANES), f32))

    def state_copy(d):
        return pltpu.make_async_remote_copy(
            src_ref=sout.at[d], dst_ref=sin.at[me], send_sem=ssend.at[d], recv_sem=srecv.at[me],
            device_id=place(d), device_id_type=MESH,
        )

    @pl.loop(1, n)
    def _(p):
        state_copy(lax.rem(me + p, n)).start()

    sin[me] = sout[me]
    loads["q2"].wait()

    @pl.loop(0, n)
    def _(d):
        @pl.when(d != me)
        def _():
            pltpu.make_async_remote_copy(
                src_ref=sout.at[d], dst_ref=sin.at[d], send_sem=ssend.at[d], recv_sem=srecv.at[d],
                device_id=place(d), device_id_type=MESH,
            ).wait_recv()

    acc[...] = jnp.zeros_like(acc)

    @pl.loop(0, chunks)
    def _(c):
        cols = wide(c)
        for j in range(WIDE // LANES):
            b = c * (WIDE // LANES) + j
            lane = slice(j * LANES, (j + 1) * LANES)
            state = []
            for r in range(modes):
                hi, low = divmod(r, SUB)
                s, row = divmod(low, part)
                o = (hi * blocks + b) * per_tile + s
                state.append(jnp.broadcast_to(sin[o, row : row + 1, :], (SUB, LANES)))
            u = p1[b] * jnp.stack(state)
            decay = a8[b]
            for m in range(rows // SUB):
                span = slice(m * SUB, (m + 1) * SUB)
                head[span, lane] = jnp.sum(u, axis=0)
                u = u * decay
        act = (q2[:, cols].astype(f32) * (y[c] + head[...])).astype(bf16)
        weight_load(w2h, w2, w2_sem, c).wait()
        acc[...] += mm(act, w2[cols, :])

    out[...] = acc[...].astype(bf16)

    @pl.when(me < n - 1)
    def _():
        @pl.loop(0, chunks)
        def _(c):
            border(c).wait_send()

    @pl.loop(0, n)
    def _(d):
        @pl.when(d != me)
        def _():
            ends_copy(d).wait_send()
            state_copy(d).wait_send()


def local(q1, k1, v1, taps, skip1, w1, q2, k2, residue, rate, skip2, w2):
    rows, channels = q1.shape
    modes = rate.shape[0]
    minor = lax.axis_size("seqmin")
    n = lax.axis_size("seqmaj") * minor
    fwd, inv = dft_tables(rows)
    operands = (q1, k1, v1, taps, skip1[None], w1, q2, k2, residue, rate, skip2[None], w2, fwd, inv)
    chunks, blocks = channels // WIDE, channels // LANES
    states = (n, modes * channels // (n * LANES), LANES)
    scratch = [pltpu.VMEM(a.shape, a.dtype) for a in operands] + [
        pltpu.VMEM((chunks, 2 * rows, WIDE), bf16),
        pltpu.VMEM((chunks, 2 * rows, WIDE), f32),
        pltpu.VMEM((chunks, 2 * rows, WIDE), f32),
        pltpu.VMEM((blocks, modes, SUB, LANES), f32),
        pltpu.VMEM((blocks, modes, SUB, LANES), f32),
        pltpu.VMEM((blocks, modes, SUB, LANES), f32),
        pltpu.VMEM((rows, WIDE), f32),
        pltpu.VMEM((rows, channels), f32),
        pltpu.VMEM((chunks, rows, WIDE), f32),
        pltpu.VMEM((chunks, rows, WIDE), bf16),
        pltpu.VMEM(states, f32),
        pltpu.VMEM(states, f32),
        pltpu.VMEM(states, f32),
        pltpu.VMEM(states, f32),
        pltpu.VMEM(states, f32),
        pltpu.SemaphoreType.DMA((12,)),
        pltpu.SemaphoreType.DMA((chunks,)),
        pltpu.SemaphoreType.DMA((chunks,)),
        pltpu.SemaphoreType.DMA((chunks,)),
        pltpu.SemaphoreType.DMA((chunks,)),
        pltpu.SemaphoreType.DMA((n,)),
        pltpu.SemaphoreType.DMA((n,)),
        pltpu.SemaphoreType.DMA((n,)),
        pltpu.SemaphoreType.DMA((n,)),
    ]
    return pl.pallas_call(
        functools.partial(kernel, n, minor),
        out_shape=jax.ShapeDtypeStruct((rows, channels), bf16),
        in_specs=[pl.BlockSpec(memory_space=pltpu.HBM)] * len(operands),
        out_specs=pl.BlockSpec(memory_space=pltpu.VMEM),
        scratch_shapes=scratch,
        compiler_params=pltpu.CompilerParams(
            collective_id=0, has_side_effects=True, vmem_limit_bytes=60 * 1024 * 1024
        ),
    )(*operands)


def solution(mesh):
    s, r = P(axes, None), P()
    specs = (s, s, s, r, r, r, s, s, r, r, r, r)
    return jax.shard_map(local, mesh=mesh, in_specs=specs, out_specs=s, check_vma=False)
```

```python
import functools

import jax
import jax.numpy as jnp
import numpy as np
from jax import lax
from jax.experimental import pallas as pl
from jax.experimental.pallas import tpu as pltpu
from jax.sharding import PartitionSpec as P

axes = ("seqmaj", "seqmin")
MESH = pl.DeviceIdType.MESH
f32, bf16 = jnp.float32, jnp.bfloat16
WIDE = 512
LANES = 128
SUB = 8


def dft_tables(rows):
    size = 2 * rows
    theta = 2.0 * np.pi * (np.arange(rows) + 0.5) / size
    angle = theta[:, None] * np.arange(size)[None, :]
    forward = np.concatenate([np.cos(angle), np.sin(angle)], axis=0)
    inverse = forward.T / rows
    return jnp.asarray(forward, bf16), jnp.asarray(inverse, bf16)


def mm(a, b):
    return jnp.dot(a, b, preferred_element_type=f32)


def spectral_product(x, h):
    half = x.shape[0] // 2
    xc, xs, hc, hs = x[:half], x[half:], h[:half], h[half:]
    return jnp.concatenate([xc * hc - xs * hs, xc * hs + xs * hc], axis=0).astype(bf16)


def kernel(
    n, minor, q1h, k1h, v1h, tapsh, skip1h, w1h, q2h, k2h, resh, rateh, skip2h, w2h, fwdh, invh, out,
    q1, k1, v1, taps, skip1, w1, q2, k2, res, rate, skip2, w2, fwd, inv,
    win, h1, h2, a8, p7, p1, head, acc, y, g2, ends, got, sout, sin, tiled_rate,
    in_sem, w1_sem, w2_sem, bsend, brecv, esend, erecv, ssend, srecv,
):
    rows, channels = q1.shape
    modes = rate.shape[0]
    chunks = channels // WIDE
    blocks = channels // LANES
    per_tile = n * SUB * LANES // (modes * channels)
    part = SUB // per_tile
    me = lax.axis_index("seqmaj") * minor + lax.axis_index("seqmin")

    def place(d):
        return (lax.div(d, minor), lax.rem(d, minor))

    def load(i, src, dst):
        return pltpu.make_async_copy(src, dst, in_sem.at[i])

    loads = {}
    for i, (name, src, dst) in enumerate([
        ("k1", k1h, k1), ("v1", v1h, v1), ("fwd", fwdh, fwd), ("taps", tapsh, taps), ("rate", rateh, rate),
        ("res", resh, res), ("inv", invh, inv), ("q1", q1h, q1), ("skip1", skip1h, skip1), ("k2", k2h, k2),
        ("skip2", skip2h, skip2), ("q2", q2h, q2),
    ]):
        loads[name] = load(i, src, dst)
        loads[name].start()

    def weight_load(src, dst, sem, c):
        span = pl.ds(pl.multiple_of(c * WIDE, WIDE), WIDE)
        return pltpu.make_async_copy(src.at[span, :], dst.at[span, :], sem.at[c])

    @pl.loop(0, chunks)
    def _(c):
        weight_load(w1h, w1, w1_sem, c).start()

    barrier = pltpu.get_barrier_semaphore()

    @pl.loop(1, n)
    def _(p):
        pl.semaphore_signal(barrier, inc=1, device_id=place(lax.rem(me + p, n)), device_id_type=MESH)

    @pl.loop(0, chunks)
    def _(c):
        weight_load(w2h, w2, w2_sem, c).start()

    def wide(c):
        return pl.ds(pl.multiple_of(c * WIDE, WIDE), WIDE)

    loads["k1"].wait()
    loads["v1"].wait()

    @pl.loop(0, chunks)
    def _(c):
        cols = wide(c)
        win[c, rows:, :] = (k1[:, cols].astype(f32) * v1[:, cols].astype(f32)).astype(bf16)

    pl.semaphore_wait(barrier, n - 1)

    def border(c):
        return pltpu.make_async_remote_copy(
            src_ref=win.at[c, pl.ds(rows, rows), :], dst_ref=win.at[c, pl.ds(0, rows), :],
            send_sem=bsend.at[c], recv_sem=brecv.at[c],
            device_id=place(lax.rem(me + 1, n)), device_id_type=MESH,
        )

    @pl.when(me < n - 1)
    def _():
        @pl.loop(0, chunks)
        def _(c):
            border(c).start()

    @pl.when(me == 0)
    def _():
        @pl.loop(0, chunks)
        def _(c):
            win[c, :rows, :] = jnp.zeros((rows, WIDE), bf16)

    loads["fwd"].wait()
    loads["taps"].wait()
    loads["rate"].wait()
    loads["res"].wait()
    step = lax.broadcasted_iota(jnp.int32, (modes, SUB, LANES), 1).astype(f32)

    def spread(ref, b):
        cols = pl.ds(pl.multiple_of(b * LANES, LANES), LANES)
        return jnp.stack([jnp.broadcast_to(ref[r : r + 1, cols], (SUB, LANES)) for r in range(modes)])

    @pl.loop(0, chunks)
    def _(c):
        h1[c] = mm(fwd[:, :rows], taps[:, wide(c)])
        for j in range(WIDE // LANES):
            b = c * (WIDE // LANES) + j
            lam = spread(rate, b)
            weight = spread(res, b) * jnp.sqrt(lam)
            decay = jnp.exp(-SUB * lam)
            a8[b] = decay
            lanes = rate[:, pl.ds(pl.multiple_of(b * LANES, LANES), LANES)]
            for hi in range(modes // SUB):
                for s in range(per_tile):
                    start = hi * SUB + s * part
                    tiled_rate[(hi * blocks + b) * per_tile + s] = lanes[start : start + part]
            p7[b] = jnp.exp(-lam * (SUB - 1.0 - step))
            p1[b] = weight * jnp.exp(-lam * (step + 1.0))
            u = weight * jnp.exp(-lam * step)
            for m in range(rows // SUB):
                head[m * SUB : (m + 1) * SUB, j * LANES : (j + 1) * LANES] = jnp.sum(u, axis=0)
                u = u * decay
        h2[c] = mm(fwd[:, :rows], head[...].astype(bf16))

    loads["inv"].wait()
    loads["q1"].wait()
    loads["skip1"].wait()
    acc[...] = jnp.zeros_like(acc)

    @pl.loop(0, chunks)
    def _(c):
        cols = wide(c)

        @pl.when(me > 0)
        def _():
            border(c).wait_recv()

        spec = spectral_product(mm(fwd[...], win[c]), h1[c])
        short = mm(inv[rows:, :], spec)
        own = win[c, rows:, :].astype(f32)
        act = (q1[:, cols].astype(f32) * (short + skip1[:, cols] * own)).astype(bf16)
        weight_load(w1h, w1, w1_sem, c).wait()
        acc[...] += mm(act, w1[cols, :])

    loads["k2"].wait()
    loads["skip2"].wait()

    def ends_copy(o):
        return pltpu.make_async_remote_copy(
            src_ref=ends.at[o], dst_ref=got.at[me], send_sem=esend.at[o], recv_sem=erecv.at[me],
            device_id=place(o), device_id_type=MESH,
        )

    @pl.loop(0, chunks)
    def _(i):
        c = lax.rem(i + me, chunks)
        cols = wide(c)
        gated = (k2[:, cols].astype(f32) * acc[:, cols].astype(bf16).astype(f32)).astype(bf16)
        g2[c] = gated
        for j in range(WIDE // LANES):
            b = c * (WIDE // LANES) + j
            g = gated[:, j * LANES : (j + 1) * LANES].astype(f32)
            decay = a8[b]
            h = jnp.broadcast_to(g[:SUB][None], (modes, SUB, LANES))
            for m in range(1, rows // SUB):
                h = h * decay + g[m * SUB : (m + 1) * SUB][None]
            e = jnp.sum(h * p7[b], axis=1)
            for hi in range(modes // SUB):
                for s in range(per_tile):
                    o = (hi * blocks + b) * per_tile + s
                    piece = e[hi * SUB + s * part : hi * SUB + (s + 1) * part]
                    ends[o] = piece

                    @pl.when(o != me)
                    def _():
                        ends_copy(o).start()

                    @pl.when(o == me)
                    def _():
                        got[me] = piece

    @pl.loop(0, chunks)
    def _(c):
        gated = g2[c]
        spec = spectral_product(mm(fwd[:, :rows], gated), h2[c])
        y[c] = mm(inv[:rows, :], spec) + skip2[:, wide(c)] * gated.astype(f32)

    @pl.loop(0, n)
    def _(d):
        @pl.when(d != me)
        def _():
            pltpu.make_async_remote_copy(
                src_ref=ends.at[d], dst_ref=got.at[d], send_sem=esend.at[d], recv_sem=erecv.at[d],
                device_id=place(d), device_id_type=MESH,
            ).wait_recv()

    own_decay = jnp.exp(-float(rows) * tiled_rate[me])

    def scan(d, state):
        sout[d] = state
        return state * own_decay + got[d]

    lax.fori_loop(0, n, scan, jnp.zeros((part, LANES), f32))

    def state_copy(d):
        return pltpu.make_async_remote_copy(
            src_ref=sout.at[d], dst_ref=sin.at[me], send_sem=ssend.at[d], recv_sem=srecv.at[me],
            device_id=place(d), device_id_type=MESH,
        )

    @pl.loop(1, n)
    def _(p):
        state_copy(lax.rem(me + p, n)).start()

    sin[me] = sout[me]
    loads["q2"].wait()

    @pl.loop(0, n)
    def _(d):
        @pl.when(d != me)
        def _():
            pltpu.make_async_remote_copy(
                src_ref=sout.at[d], dst_ref=sin.at[d], send_sem=ssend.at[d], recv_sem=srecv.at[d],
                device_id=place(d), device_id_type=MESH,
            ).wait_recv()

    acc[...] = jnp.zeros_like(acc)

    @pl.loop(0, chunks)
    def _(c):
        cols = wide(c)
        for j in range(WIDE // LANES):
            b = c * (WIDE // LANES) + j
            lane = slice(j * LANES, (j + 1) * LANES)
            state = []
            for r in range(modes):
                hi, low = divmod(r, SUB)
                s, row = divmod(low, part)
                o = (hi * blocks + b) * per_tile + s
                state.append(jnp.broadcast_to(sin[o, row : row + 1, :], (SUB, LANES)))
            u = p1[b] * jnp.stack(state)
            decay = a8[b]
            for m in range(rows // SUB):
                span = slice(m * SUB, (m + 1) * SUB)
                head[span, lane] = jnp.sum(u, axis=0)
                u = u * decay
        act = (q2[:, cols].astype(f32) * (y[c] + head[...])).astype(bf16)
        weight_load(w2h, w2, w2_sem, c).wait()
        acc[...] += mm(act, w2[cols, :])

    out[...] = acc[...].astype(bf16)

    @pl.when(me < n - 1)
    def _():
        @pl.loop(0, chunks)
        def _(c):
            border(c).wait_send()

    @pl.loop(0, n)
    def _(d):
        @pl.when(d != me)
        def _():
            ends_copy(d).wait_send()
            state_copy(d).wait_send()


def local(q1, k1, v1, taps, skip1, w1, q2, k2, residue, rate, skip2, w2):
    rows, channels = q1.shape
    modes = rate.shape[0]
    minor = lax.axis_size("seqmin")
    n = lax.axis_size("seqmaj") * minor
    fwd, inv = dft_tables(rows)
    operands = (q1, k1, v1, taps, skip1[None], w1, q2, k2, residue, rate, skip2[None], w2, fwd, inv)
    chunks, blocks = channels // WIDE, channels // LANES
    states = (n, modes * channels // (n * LANES), LANES)
    scratch = [pltpu.VMEM(a.shape, a.dtype) for a in operands] + [
        pltpu.VMEM((chunks, 2 * rows, WIDE), bf16),
        pltpu.VMEM((chunks, 2 * rows, WIDE), f32),
        pltpu.VMEM((chunks, 2 * rows, WIDE), f32),
        pltpu.VMEM((blocks, modes, SUB, LANES), f32),
        pltpu.VMEM((blocks, modes, SUB, LANES), f32),
        pltpu.VMEM((blocks, modes, SUB, LANES), f32),
        pltpu.VMEM((rows, WIDE), f32),
        pltpu.VMEM((rows, channels), f32),
        pltpu.VMEM((chunks, rows, WIDE), f32),
        pltpu.VMEM((chunks, rows, WIDE), bf16),
        pltpu.VMEM(states, f32),
        pltpu.VMEM(states, f32),
        pltpu.VMEM(states, f32),
        pltpu.VMEM(states, f32),
        pltpu.VMEM(states, f32),
        pltpu.SemaphoreType.DMA((12,)),
        pltpu.SemaphoreType.DMA((chunks,)),
        pltpu.SemaphoreType.DMA((chunks,)),
        pltpu.SemaphoreType.DMA((chunks,)),
        pltpu.SemaphoreType.DMA((chunks,)),
        pltpu.SemaphoreType.DMA((n,)),
        pltpu.SemaphoreType.DMA((n,)),
        pltpu.SemaphoreType.DMA((n,)),
        pltpu.SemaphoreType.DMA((n,)),
    ]
    return pl.pallas_call(
        functools.partial(kernel, n, minor),
        out_shape=jax.ShapeDtypeStruct((rows, channels), bf16),
        in_specs=[pl.BlockSpec(memory_space=pltpu.HBM)] * len(operands),
        out_specs=pl.BlockSpec(memory_space=pltpu.VMEM),
        scratch_shapes=scratch,
        compiler_params=pltpu.CompilerParams(
            collective_id=0, has_side_effects=True, vmem_limit_bytes=60 * 1024 * 1024
        ),
    )(*operands)


def solution(mesh):
    s, r = P(axes, None), P()
    specs = (s, s, s, r, r, r, s, s, r, r, r, r)
    return jax.shard_map(local, mesh=mesh, in_specs=specs, out_specs=s, check_vma=False)
```

```python
import functools

import jax
import jax.numpy as jnp
import numpy as np
from jax import lax
from jax.experimental import pallas as pl
from jax.experimental.pallas import tpu as pltpu
from jax.sharding import PartitionSpec as P

axes = ("seqmaj", "seqmin")
MESH = pl.DeviceIdType.MESH
f32, bf16 = jnp.float32, jnp.bfloat16
WIDE = 512
LANES = 128
SUB = 8


def dft_tables(rows):
    size = 2 * rows
    theta = 2.0 * np.pi * (np.arange(rows) + 0.5) / size
    angle = theta[:, None] * np.arange(size)[None, :]
    forward = np.concatenate([np.cos(angle), np.sin(angle)], axis=0)
    inverse = forward.T / rows
    return jnp.asarray(forward, bf16), jnp.asarray(inverse, bf16)


def mm(a, b):
    return jnp.dot(a, b, preferred_element_type=f32)


def spectral_product(x, h):
    half = x.shape[0] // 2
    xc, xs, hc, hs = x[:half], x[half:], h[:half], h[half:]
    return jnp.concatenate([xc * hc - xs * hs, xc * hs + xs * hc], axis=0).astype(bf16)


def kernel(
    n, minor, q1h, k1h, v1h, tapsh, skip1h, w1h, q2h, k2h, resh, rateh, skip2h, w2h, fwdh, invh, out,
    q1, k1, v1, taps, skip1, w1, q2, k2, res, rate, skip2, w2, fwd, inv,
    win, h1, h2, a8, p7, p1, head, acc, y, g2, ends, got, sout, sin, tiled_rate,
    in_sem, w1_sem, w2_sem, bsend, brecv, esend, erecv, ssend, srecv,
):
    rows, channels = q1.shape
    modes = rate.shape[0]
    chunks = channels // WIDE
    blocks = channels // LANES
    per_tile = n * SUB * LANES // (modes * channels)
    part = SUB // per_tile
    me = lax.axis_index("seqmaj") * minor + lax.axis_index("seqmin")

    def place(d):
        return (lax.div(d, minor), lax.rem(d, minor))

    def load(i, src, dst):
        return pltpu.make_async_copy(src, dst, in_sem.at[i])

    loads = {}
    for i, (name, src, dst) in enumerate([
        ("k1", k1h, k1), ("v1", v1h, v1), ("fwd", fwdh, fwd), ("taps", tapsh, taps), ("rate", rateh, rate),
        ("res", resh, res), ("inv", invh, inv), ("q1", q1h, q1), ("skip1", skip1h, skip1), ("k2", k2h, k2),
        ("skip2", skip2h, skip2), ("q2", q2h, q2),
    ]):
        loads[name] = load(i, src, dst)
        loads[name].start()

    def weight_load(src, dst, sem, c):
        span = pl.ds(pl.multiple_of(c * WIDE, WIDE), WIDE)
        return pltpu.make_async_copy(src.at[span, :], dst.at[span, :], sem.at[c])

    @pl.loop(0, chunks)
    def _(c):
        weight_load(w1h, w1, w1_sem, c).start()

    barrier = pltpu.get_barrier_semaphore()

    @pl.loop(1, n)
    def _(p):
        pl.semaphore_signal(barrier, inc=1, device_id=place(lax.rem(me + p, n)), device_id_type=MESH)

    @pl.loop(0, chunks)
    def _(c):
        weight_load(w2h, w2, w2_sem, c).start()

    def wide(c):
        return pl.ds(pl.multiple_of(c * WIDE, WIDE), WIDE)

    loads["k1"].wait()
    loads["v1"].wait()

    @pl.loop(0, chunks)
    def _(c):
        cols = wide(c)
        win[c, rows:, :] = (k1[:, cols].astype(f32) * v1[:, cols].astype(f32)).astype(bf16)

    pl.semaphore_wait(barrier, n - 1)

    def border(c):
        return pltpu.make_async_remote_copy(
            src_ref=win.at[c, pl.ds(rows, rows), :], dst_ref=win.at[c, pl.ds(0, rows), :],
            send_sem=bsend.at[c], recv_sem=brecv.at[c],
            device_id=place(lax.rem(me + 1, n)), device_id_type=MESH,
        )

    @pl.when(me < n - 1)
    def _():
        @pl.loop(0, chunks)
        def _(c):
            border(c).start()

    @pl.when(me == 0)
    def _():
        @pl.loop(0, chunks)
        def _(c):
            win[c, :rows, :] = jnp.zeros((rows, WIDE), bf16)

    loads["fwd"].wait()
    loads["taps"].wait()
    loads["rate"].wait()
    loads["res"].wait()
    step = lax.broadcasted_iota(jnp.int32, (modes, SUB, LANES), 1).astype(f32)

    def spread(ref, b):
        cols = pl.ds(pl.multiple_of(b * LANES, LANES), LANES)
        return jnp.stack([jnp.broadcast_to(ref[r : r + 1, cols], (SUB, LANES)) for r in range(modes)])

    @pl.loop(0, chunks)
    def _(c):
        h1[c] = mm(fwd[:, :rows], taps[:, wide(c)])
        for j in range(WIDE // LANES):
            b = c * (WIDE // LANES) + j
            lam = spread(rate, b)
            weight = spread(res, b) * jnp.sqrt(lam)
            decay = jnp.exp(-SUB * lam)
            a8[b] = decay
            lanes = rate[:, pl.ds(pl.multiple_of(b * LANES, LANES), LANES)]
            for hi in range(modes // SUB):
                for s in range(per_tile):
                    start = hi * SUB + s * part
                    tiled_rate[(hi * blocks + b) * per_tile + s] = lanes[start : start + part]
            p7[b] = jnp.exp(-lam * (SUB - 1.0 - step))
            p1[b] = weight * jnp.exp(-lam * (step + 1.0))
            u = weight * jnp.exp(-lam * step)
            for m in range(rows // SUB):
                head[m * SUB : (m + 1) * SUB, j * LANES : (j + 1) * LANES] = jnp.sum(u, axis=0)
                u = u * decay
        h2[c] = mm(fwd[:, :rows], head[...].astype(bf16))

    loads["inv"].wait()
    loads["q1"].wait()
    loads["skip1"].wait()
    acc[...] = jnp.zeros_like(acc)

    @pl.loop(0, chunks)
    def _(c):
        cols = wide(c)

        @pl.when(me > 0)
        def _():
            border(c).wait_recv()

        spec = spectral_product(mm(fwd[...], win[c]), h1[c])
        short = mm(inv[rows:, :], spec)
        own = win[c, rows:, :].astype(f32)
        act = (q1[:, cols].astype(f32) * (short + skip1[:, cols] * own)).astype(bf16)
        weight_load(w1h, w1, w1_sem, c).wait()
        acc[...] += mm(act, w1[cols, :])

    loads["k2"].wait()
    loads["skip2"].wait()

    def all_tiles(src, dst, send_sem, recv_sem):
        others = pl.ds(0, n - 1)
        return pltpu.make_async_remote_copy(
            src_ref=src.at[others], dst_ref=dst.at[others], send_sem=send_sem.at[0], recv_sem=recv_sem.at[0],
            device_id=place(lax.rem(me + 1, n)), device_id_type=MESH,
        )

    def ends_copy(o):
        return pltpu.make_async_remote_copy(
            src_ref=ends.at[o], dst_ref=got.at[me], send_sem=esend.at[0], recv_sem=erecv.at[0],
            device_id=place(o), device_id_type=MESH,
        )

    @pl.loop(0, chunks)
    def _(i):
        c = lax.rem(i + me, chunks)
        cols = wide(c)
        gated = (k2[:, cols].astype(f32) * acc[:, cols].astype(bf16).astype(f32)).astype(bf16)
        g2[c] = gated
        for j in range(WIDE // LANES):
            b = c * (WIDE // LANES) + j
            g = gated[:, j * LANES : (j + 1) * LANES].astype(f32)
            decay = a8[b]
            h = jnp.broadcast_to(g[:SUB][None], (modes, SUB, LANES))
            for m in range(1, rows // SUB):
                h = h * decay + g[m * SUB : (m + 1) * SUB][None]
            e = jnp.sum(h * p7[b], axis=1)
            for hi in range(modes // SUB):
                for s in range(per_tile):
                    o = (hi * blocks + b) * per_tile + s
                    piece = e[hi * SUB + s * part : hi * SUB + (s + 1) * part]
                    ends[o] = piece

                    @pl.when(o != me)
                    def _():
                        ends_copy(o).start()

                    @pl.when(o == me)
                    def _():
                        got[me] = piece

    @pl.loop(0, chunks)
    def _(c):
        gated = g2[c]
        spec = spectral_product(mm(fwd[:, :rows], gated), h2[c])
        y[c] = mm(inv[:rows, :], spec) + skip2[:, wide(c)] * gated.astype(f32)

    all_tiles(ends, got, esend, erecv).wait_recv()

    own_decay = jnp.exp(-float(rows) * tiled_rate[me])

    def scan(d, state):
        sout[d] = state
        return state * own_decay + got[d]

    lax.fori_loop(0, n, scan, jnp.zeros((part, LANES), f32))

    def state_copy(d):
        return pltpu.make_async_remote_copy(
            src_ref=sout.at[d], dst_ref=sin.at[me], send_sem=ssend.at[0], recv_sem=srecv.at[0],
            device_id=place(d), device_id_type=MESH,
        )

    @pl.loop(1, n)
    def _(p):
        state_copy(lax.rem(me + p, n)).start()

    sin[me] = sout[me]
    loads["q2"].wait()

    all_tiles(sout, sin, ssend, srecv).wait_recv()

    acc[...] = jnp.zeros_like(acc)

    @pl.loop(0, chunks)
    def _(c):
        cols = wide(c)
        for j in range(WIDE // LANES):
            b = c * (WIDE // LANES) + j
            lane = slice(j * LANES, (j + 1) * LANES)
            state = []
            for r in range(modes):
                hi, low = divmod(r, SUB)
                s, row = divmod(low, part)
                o = (hi * blocks + b) * per_tile + s
                state.append(jnp.broadcast_to(sin[o, row : row + 1, :], (SUB, LANES)))
            u = p1[b] * jnp.stack(state)
            decay = a8[b]
            for m in range(rows // SUB):
                span = slice(m * SUB, (m + 1) * SUB)
                head[span, lane] = jnp.sum(u, axis=0)
                u = u * decay
        act = (q2[:, cols].astype(f32) * (y[c] + head[...])).astype(bf16)
        weight_load(w2h, w2, w2_sem, c).wait()
        acc[...] += mm(act, w2[cols, :])

    out[...] = acc[...].astype(bf16)

    @pl.when(me < n - 1)
    def _():
        @pl.loop(0, chunks)
        def _(c):
            border(c).wait_send()

    all_tiles(ends, got, esend, erecv).wait_send()
    all_tiles(sout, sin, ssend, srecv).wait_send()


def local(q1, k1, v1, taps, skip1, w1, q2, k2, residue, rate, skip2, w2):
    rows, channels = q1.shape
    modes = rate.shape[0]
    minor = lax.axis_size("seqmin")
    n = lax.axis_size("seqmaj") * minor
    fwd, inv = dft_tables(rows)
    operands = (q1, k1, v1, taps, skip1[None], w1, q2, k2, residue, rate, skip2[None], w2, fwd, inv)
    chunks, blocks = channels // WIDE, channels // LANES
    states = (n, modes * channels // (n * LANES), LANES)
    scratch = [pltpu.VMEM(a.shape, a.dtype) for a in operands] + [
        pltpu.VMEM((chunks, 2 * rows, WIDE), bf16),
        pltpu.VMEM((chunks, 2 * rows, WIDE), f32),
        pltpu.VMEM((chunks, 2 * rows, WIDE), f32),
        pltpu.VMEM((blocks, modes, SUB, LANES), f32),
        pltpu.VMEM((blocks, modes, SUB, LANES), f32),
        pltpu.VMEM((blocks, modes, SUB, LANES), f32),
        pltpu.VMEM((rows, WIDE), f32),
        pltpu.VMEM((rows, channels), f32),
        pltpu.VMEM((chunks, rows, WIDE), f32),
        pltpu.VMEM((chunks, rows, WIDE), bf16),
        pltpu.VMEM(states, f32),
        pltpu.VMEM(states, f32),
        pltpu.VMEM(states, f32),
        pltpu.VMEM(states, f32),
        pltpu.VMEM(states, f32),
        pltpu.SemaphoreType.DMA((12,)),
        pltpu.SemaphoreType.DMA((chunks,)),
        pltpu.SemaphoreType.DMA((chunks,)),
        pltpu.SemaphoreType.DMA((chunks,)),
        pltpu.SemaphoreType.DMA((chunks,)),
        pltpu.SemaphoreType.DMA((1,)),
        pltpu.SemaphoreType.DMA((1,)),
        pltpu.SemaphoreType.DMA((1,)),
        pltpu.SemaphoreType.DMA((1,)),
    ]
    return pl.pallas_call(
        functools.partial(kernel, n, minor),
        out_shape=jax.ShapeDtypeStruct((rows, channels), bf16),
        in_specs=[pl.BlockSpec(memory_space=pltpu.HBM)] * len(operands),
        out_specs=pl.BlockSpec(memory_space=pltpu.VMEM),
        scratch_shapes=scratch,
        compiler_params=pltpu.CompilerParams(
            collective_id=0, has_side_effects=True, vmem_limit_bytes=60 * 1024 * 1024
        ),
    )(*operands)


def solution(mesh):
    s, r = P(axes, None), P()
    specs = (s, s, s, r, r, r, s, s, r, r, r, r)
    return jax.shard_map(local, mesh=mesh, in_specs=specs, out_specs=s, check_vma=False)
```
